32 devices in a mesh: orb: 8 (over y, x, core), aux: 4 (over z).
Axes of the slice: x: 2, y: 2, z: 4, core: 2. Of those that a mesh axis runs over, the one named last changes fastest.
Arguments:
- blocks: bfloat16 [32, 256, 6144], P('orb', None, 'aux'), may hold values from -0.65625 to 0.65625
- excitation: float32 [32, 256], replicated, may hold values from 0.5 to 8
- partner: int32 [8, 8], replicated, may hold values from 0 to 3
- neighbours: int32 [8, 8], replicated, may hold values from 0 to 1, as said below
Outputs:
- gradient: bfloat16 [32, 256, 6144], P('orb', None, 'aux')
The draws below stay inside these ranges and needn't reach their ends.
Inputs may be any that keep to these rules, and one draw needn't show every extreme that they name: neighbours is symmetric: neighbours[d][s] equals neighbours[s][d].
All inputs are finite; a program needn't handle non-finite values.
Results may differ from the reference program's by a relative error of at most 0.0048.
Values may be sent and summed in bfloat16 or wider, within the bound.
No kernel may reach another device: no remote copies, remote signals or barrier semaphores. Data moves between devices by JAX's collectives and lax.ppermute only.
A program may use at most 192 MiB of HBM per device.

```python
import math
import jax
import jax.numpy as jnp
from jax import lax

NV = 256
NAUX = 6144
ORB_DEV = 4
NOCC = 32
N_ORB = 8


def draw_neighbours(key, part):
    coins = jax.random.randint(key, (N_ORB, N_ORB), 0, 2).astype(jnp.int32)
    row_index = lax.broadcasted_iota(jnp.int32, (N_ORB, N_ORB), 0)
    col_index = lax.broadcasted_iota(jnp.int32, (N_ORB, N_ORB), 1)
    return jnp.where(row_index <= col_index, coins, coins.T).astype(jnp.int32)


def place_ends(entries, rng, smallest, top_value):
    longest = entries.shape.index(max(entries.shape))
    spots = []
    for shift in (0, 1):
        where = [jax.random.randint(jax.random.fold_in(rng, axis), (), 0, length) for axis, length in enumerate(entries.shape)]
        where[longest] = (where[longest] + shift) % entries.shape[longest]
        spots.append(tuple(where))
    return entries.at[spots[0]].set(smallest).at[spots[1]].set(top_value)


def level_of(own_key, dims, split, smallest, largest):
    loudness, own = 1.0, jax.random.fold_in(own_key, 6)
    for axis_at, parts in split:
        draws = jnp.exp(jax.random.uniform(jax.random.fold_in(own, axis_at), (parts,), jnp.float32, smallest / len(split), largest / len(split)))
        loudness = loudness * jnp.repeat(draws, dims[axis_at] // parts).reshape([-1 if axis == axis_at else 1 for axis in range(len(dims))])
    return loudness


def scatter_about(key, dims, deviation, most, pieces=(), kind=jnp.bfloat16):
    result = jax.random.normal(key, dims, jnp.float32) * deviation
    if len(pieces) > 0:
        result = level_of(key, dims, pieces, -0.22, 0.18) * result
    return jnp.clip(result, min=-most, max=most).astype(kind)


def setup_inputs(seed: int = 0) -> dict:
    seeds = jax.random.split(jax.random.key(seed), 5)
    return {
        "blocks": scatter_about(seeds[0], (NOCC, NV, NAUX), 0.11, 0.65625, ((0, 8), (2, 4))),
        "excitation": jnp.clip(jnp.exp(jax.random.uniform(seeds[1], (NOCC, NV), jnp.float32, math.log(0.5), math.log(8.0))), 0.5, 8.0),
        "partner": place_ends(jax.random.randint(seeds[2], (N_ORB, N_ORB), 0, ORB_DEV), jax.random.fold_in(seeds[2], 1), 0, ORB_DEV - 1).astype(jnp.int32),
        "neighbours": draw_neighbours(jax.random.fold_in(seeds[4], 71), 0),
    }


def reference(blocks, excitation, partner, neighbours):
    def one_device(anchor):
        wanted = partner[:, anchor]
        own_rows = (anchor * ORB_DEV + wanted).astype(jnp.int32)
        far_rows = (jnp.arange(N_ORB, dtype=jnp.int32) * ORB_DEV + partner[anchor, :]).astype(jnp.int32)
        own_blocks = blocks[own_rows].astype(jnp.float32)
        far_blocks = blocks[far_rows].astype(jnp.float32)
        kernel = jnp.einsum("sap,sbp->sab", own_blocks, far_blocks)
        weights = neighbours[anchor, :].astype(jnp.float32)
        denominator = excitation[own_rows][:, :, None] + excitation[far_rows][:, None, :]
        amplitude = (-weights[:, None, None] * kernel / denominator).astype(jnp.bfloat16)
        product = jnp.einsum("sab,sbp->sap", amplitude.astype(jnp.float32), far_blocks)
        onehot = (wanted[:, None] == jnp.arange(ORB_DEV, dtype=jnp.int32)[None, :]).astype(jnp.float32)
        summed = jnp.einsum("si,sap->iap", onehot, product, precision=lax.Precision.HIGHEST)
        return summed.astype(jnp.bfloat16)

    stacked = lax.map(one_device, jnp.arange(N_ORB, dtype=jnp.int32))
    return stacked.reshape(NOCC, NV, NAUX)
```

```python
import jax
import jax.numpy as jnp
from jax import lax
from jax.experimental import pallas as pl
from jax.experimental.pallas import tpu as pltpu
from jax.sharding import PartitionSpec as P

VMEM_BYTES = 56 * 1024 * 1024
WINDOW = 2
SMALL = pl.CostEstimate(flops=1, transcendentals=0, bytes_accessed=1)
LARGE = pl.CostEstimate(flops=1, transcendentals=0, bytes_accessed=60_000_000)
PARAMS = pltpu.CompilerParams(vmem_limit_bytes=VMEM_BYTES)


def forward_steps(peers):
    if peers == 8:
        ring = [0, 1, 3, 2]
        around = []
        for d in range(peers):
            place = ring.index(d >> 1)
            turn = 1 if d & 1 == 0 else 3
            around.append(ring[(place + turn) % 4] * 2 + (d & 1))
        crossed = [d ^ (3 if d & 1 == 0 else 5) for d in range(peers)]
        return [[d ^ (6 if d & 4 == 0 else 7) for d in range(peers)], crossed, around]
    steps = []
    for step in range(2, peers, 2):
        top = 1 << (step.bit_length() - 1)
        steps.append([d ^ (step if d & top == 0 else step + 1) for d in range(peers)])
    return steps


def inverse(step):
    back = [0] * len(step)
    for source, target in enumerate(step):
        back[target] = source
    return back


def after(array, *others):
    return lax.optimization_barrier((array, *others))[0]


def own_of(plan, column):
    return plan[2 + 3 * column]


def pick(blocks, partner, neighbours, rows, plan, columns, cost=SMALL):
    local_count, width, depth = blocks.shape
    count = len(columns)

    def lookup(row, index):
        value = row[0]
        for place, entry in enumerate(row[1:], 1):
            value = jnp.where(index == place, entry, value)
        return value

    def body(*refs):
        if plan is None:
            partners, kept, source = refs[:3]
            outs, made, into = refs[3 : 3 + count], refs[3 + count], refs[-1]
            me = lax.axis_index("orb").astype(jnp.int32)
            made[0] = me
            made[1] = lax.axis_index("aux").astype(jnp.int32)
            others = [lookup(row, me) for row in rows]
            for column in columns:
                made[2 + 3 * column] = partners[others[column], me]
        else:
            made, source = refs[:2]
            outs, into = refs[2 : 2 + count], refs[-1]
        reads = []
        for number, column in enumerate(columns):
            reads.append(
                pltpu.make_async_copy(
                    source.at[own_of(made, column)], outs[number], into.at[number]
                )
            )
        for read in reads:
            read.start()
        if plan is None:
            for column, other in enumerate(others):
                made[2 + 3 * column] = partners[other, me]
                made[3 + 3 * column] = other * local_count + partners[me, other]
                made[4 + 3 * column] = kept[me, other]
        for read in reads:
            read.wait()

    anywhere = pl.BlockSpec(memory_space=pl.ANY)
    out_specs = [pl.BlockSpec(memory_space=pltpu.VMEM)] * count
    out_shape = [jax.ShapeDtypeStruct((width, depth), blocks.dtype)] * count
    if plan is None:
        out_specs.append(pl.BlockSpec(memory_space=pltpu.SMEM))
        out_shape.append(jax.ShapeDtypeStruct((2 + 3 * len(rows),), jnp.int32))
    scalars = (partner, neighbours) if plan is None else (plan,)
    return pl.pallas_call(
        body,
        grid_spec=pltpu.PrefetchScalarGridSpec(
            num_scalar_prefetch=len(scalars),
            in_specs=[anywhere],
            out_specs=out_specs,
            scratch_shapes=[pltpu.SemaphoreType.DMA((count,))],
        ),
        out_shape=out_shape,
        compiler_params=PARAMS,
        cost_estimate=cost,
        name="pick",
    )(*scalars, blocks)


def kernel_parts(own, far, shards, sent):
    width, depth = own[0].shape
    rows = width // shards
    pairs = len(own)
    arrived = [block for block in far if block is not None]

    def body(*refs):
        owns, others = refs[:pairs], list(refs[pairs : pairs + len(arrived)])
        outs, full = refs[pairs + len(arrived) : -1], refs[-1]
        turn = lax.axis_index("aux").astype(jnp.int32)
        for pair in range(pairs):
            other = owns[pair] if far[pair] is None else others.pop(0)
            full[...] = lax.dot_general(
                owns[pair][...],
                other[...],
                (((1,), (1,)), ((), ())),
                preferred_element_type=jnp.float32,
            )
            for j in range(shards):
                start = pl.multiple_of(lax.rem(turn + j, shards) * rows, rows)
                outs[j][pair] = full[pl.ds(start, rows), :].astype(outs[j].dtype)

    return pl.pallas_call(
        body,
        out_shape=[
            jax.ShapeDtypeStruct((pairs, rows, width), sent if j else jnp.float32)
            for j in range(shards)
        ],
        scratch_shapes=[pltpu.VMEM((width, width), jnp.float32)],
        compiler_params=PARAMS,
        cost_estimate=SMALL,
        name="kernel_parts",
    )(*own, *arrived)


def denominators(excitation, plan, column_groups, shards, local_count):
    width = excitation.shape[1]
    rows = width // shards
    count = len(column_groups)

    def body(plan, energies, *refs):
        outs, turned = refs[:count], refs[count]
        turned[...] = energies[...].T
        own_part = turned[pl.ds(pl.multiple_of(plan[1] * rows, rows), rows), :]
        lane = lax.broadcasted_iota(jnp.int32, own_part.shape, 1)
        for out, columns in zip(outs, column_groups):
            for pair, column in enumerate(columns):
                own = plan[0] * local_count + own_of(plan, column)
                left = jnp.sum(jnp.where(lane == own, own_part, 0.0), axis=1, keepdims=True)
                right = energies[pl.ds(plan[3 + 3 * column], 1), :]
                kept = plan[4 + 3 * column].astype(jnp.float32)
                out[pair] = jnp.where(kept > 0, left + right, jnp.inf)

    shapes = [(len(columns), rows, width) for columns in column_groups]
    return pl.pallas_call(
        body,
        grid_spec=pltpu.PrefetchScalarGridSpec(
            num_scalar_prefetch=1,
            grid=(1,),
            in_specs=[pl.BlockSpec(excitation.shape, lambda i, plan: (0, 0))],
            out_specs=[pl.BlockSpec(shape, lambda i, plan: (0, 0, 0)) for shape in shapes],
            scratch_shapes=[pltpu.VMEM(excitation.shape[::-1], jnp.float32)],
        ),
        out_shape=[jax.ShapeDtypeStruct(shape, jnp.float32) for shape in shapes],
        cost_estimate=SMALL,
        name="denominators",
    )(plan, excitation)


def amplitudes(parts, denominator):
    kernel = parts[0]
    for part in parts[1:]:
        kernel = kernel + part.astype(jnp.float32)
    return (-kernel / denominator).astype(jnp.bfloat16)


def assemble(shard_refs, pair, turn, scratch, shards):
    rows = shard_refs[0].shape[1]
    for j in range(shards):
        start = pl.multiple_of(lax.rem(turn + shards - j, shards) * rows, rows)
        scratch[pl.ds(start, rows), :] = shard_refs[j][pair]


def whole_spec(array):
    zeros = (0,) * array.ndim
    return pl.BlockSpec(array.shape, lambda i, plan: zeros)


def accumulate(blocks, before, items, groups, plan, shards, kind):
    local_count, width, depth = blocks.shape
    pairs = len(items)
    step = 512 if depth % 512 == 0 and pairs < 16 else 256
    arrived = [item[0] for item in items if item[0] is not None]
    local = len(arrived) < pairs
    flat = [shard for group in groups for shard in group]

    def body(plan, *refs):
        refs = list(refs)
        own_ref = refs.pop(0) if local else None
        sums = None if before is None else refs.pop(0)
        others = [refs.pop(0) for _ in arrived]
        held = [[refs.pop(0) for _ in group] for group in groups]
        out, total, amps, spare = refs

        @pl.when(pl.program_id(0) == 0)
        def _():
            for number, (block, column, group, pair, transposed) in enumerate(items):
                if transposed:
                    assemble(held[group], pair, plan[1], spare, shards)
                    amps[number] = spare[...].T
                else:
                    assemble(held[group], pair, plan[1], amps.at[number], shards)

        total[...] = jnp.zeros_like(total) if sums is None else sums[...]
        for number, (block, column, group, pair, transposed) in enumerate(items):
            factor = own_ref[0] if block is None else others.pop(0)[...]
            total[own_of(plan, column)] += jnp.dot(
                amps[number], factor, preferred_element_type=jnp.float32
            )
        out[...] = total[...].astype(out.dtype)

    own_spec = pl.BlockSpec((1, width, step), lambda i, plan: (own_of(plan, 0), 0, i))
    far_spec = pl.BlockSpec((width, step), lambda i, plan: (0, i))
    all_spec = pl.BlockSpec((local_count, width, step), lambda i, plan: (0, 0, i))
    return pl.pallas_call(
        body,
        grid_spec=pltpu.PrefetchScalarGridSpec(
            num_scalar_prefetch=1,
            grid=(depth // step,),
            in_specs=[own_spec] * local
            + [all_spec] * (before is not None)
            + [far_spec] * len(arrived)
            + [whole_spec(shard) for shard in flat],
            out_specs=all_spec,
            scratch_shapes=[
                pltpu.VMEM((local_count, width, step), jnp.float32),
                pltpu.VMEM((pairs, width, width), jnp.bfloat16),
                pltpu.VMEM((width, width), jnp.bfloat16),
            ],
        ),
        out_shape=jax.ShapeDtypeStruct(blocks.shape, kind),
        compiler_params=PARAMS,
        cost_estimate=SMALL,
        name="accumulate",
    )(
        plan,
        *([blocks] if local else []),
        *([] if before is None else [before]),
        *arrived,
        *flat,
    )


def on_device(blocks, excitation, partner, neighbours):
    peers = lax.axis_size("orb")
    shards = lax.axis_size("aux")
    local_count = blocks.shape[0]
    forward = forward_steps(peers)
    count = len(forward)
    backward = [inverse(step) for step in forward]
    mate = [d ^ 1 for d in range(peers)]
    from_step = [2 + i for i in range(count)]
    to_step = [2 + count + i for i in range(count)]
    rows = [list(range(peers)), mate] + backward + forward
    def around(array, shift):
        return lax.ppermute(array, "aux", [(i, (i + shift) % shards) for i in range(shards)])

    def send(array, step):
        return lax.ppermute(array, "orb", list(enumerate(step)))

    moves, columns = [mate, forward[0]], [1, to_step[0]]
    for i in range(1, count):
        moves += [forward[i], backward[i]]
        columns += [to_step[i], from_step[i]]
    moves.append(backward[0])
    columns.append(from_step[0])
    picked = pick(blocks, partner, neighbours, rows, None, [*columns[:3], 0])
    *picked, local, plan = picked
    picked += pick(blocks, None, None, rows, plan, columns[3:])
    own = dict(zip([*columns, 0], [*picked, local]))

    size = 1 if count <= 3 else 4
    step_groups = [list(range(i, min(i + size, count))) for i in range(1, count, size)]
    column_groups = [[0, 1], [from_step[0]]]
    for steps in step_groups:
        column_groups.append([c for i in steps for c in (from_step[i], to_step[i])])
    energies = denominators(excitation, plan, column_groups, shards, local_count)

    def reduced(far, columns, sent):
        parts = kernel_parts([own[column] for column in columns], far, shards, sent)
        return parts, [parts[0]] + [around(parts[j], j) for j in range(1, shards)]

    def spread(array):
        return [array] + [around(array, j) for j in range(1, shards)]

    received = [send(picked[number], moves[number]) for number in range(3)]

    def move(*gates):
        number = len(received)
        block = after(picked[number], received[number - WINDOW], *gates)
        received.append(send(block, moves[number]))

    parts, held = reduced([None, received[0]], [0, 1], jnp.float32)
    local = amplitudes(held, energies[0])
    move(*held[1:], *energies, *picked)
    far = after(received[1], local, *energies, *picked)
    parts, held = reduced([far], [from_step[0]], jnp.bfloat16)
    mine = amplitudes(held, energies[1])
    theirs = send(mine, backward[0])
    groups = [spread(after(local, *held[1:]))]
    move(theirs)
    waiting = [mine, theirs]
    items = [
        (None, 0, 0, 0, False),
        (received[0], 1, 0, 1, False),
        (received[1], from_step[0], 1, 0, False),
        (None, to_step[0], 1, 1, True),
    ]
    gates = groups[0][1:]
    for number, steps in enumerate(step_groups):
        columns = column_groups[2 + number]
        while len(received) < 2 + 2 * steps[-1]:
            move()
        far = [block for i in steps for block in received[2 * i : 2 * i + 2]]
        far = [after(block, *gates) for block in far]
        parts, held = reduced(far, columns, jnp.bfloat16)
        while len(received) < len(moves) - 1:
            move()
        amplitude = amplitudes(held, energies[2 + number])
        if number == 0:
            move(amplitude)
        for place, column in enumerate(columns):
            items.append((far[place], column, 1 + number, len(waiting) + place, False))
        group = jnp.concatenate([*waiting, amplitude])
        groups.append(spread(group))
        waiting = []
        gates = [group]
    items[3] = (received[-1], *items[3][1:])
    items = items[:3] + items[4:] + [items[3]]
    return accumulate(blocks, None, items, groups, plan, shards, jnp.bfloat16)


def solution(mesh):
    placed = (P("orb", None, "aux"), P(), P(), P())
    return jax.shard_map(
        on_device, mesh=mesh, in_specs=placed, out_specs=P("orb", None, "aux"), check_vma=False
    )
```

```python
import jax
import jax.numpy as jnp
from jax import lax
from jax.experimental import pallas as pl
from jax.experimental.pallas import tpu as pltpu
from jax.sharding import PartitionSpec as P

VMEM_BYTES = 56 * 1024 * 1024
WINDOW = 2
SMALL = pl.CostEstimate(flops=1, transcendentals=0, bytes_accessed=1)
LARGE = pl.CostEstimate(flops=1, transcendentals=0, bytes_accessed=60_000_000)
PARAMS = pltpu.CompilerParams(vmem_limit_bytes=VMEM_BYTES)


def forward_steps(peers):
    if peers == 8:
        ring = [0, 1, 3, 2]
        around = []
        for d in range(peers):
            place = ring.index(d >> 1)
            turn = 1 if d & 1 == 0 else 3
            around.append(ring[(place + turn) % 4] * 2 + (d & 1))
        crossed = [d ^ (3 if d & 1 == 0 else 5) for d in range(peers)]
        return [[d ^ (6 if d & 4 == 0 else 7) for d in range(peers)], crossed, around]
    steps = []
    for step in range(2, peers, 2):
        top = 1 << (step.bit_length() - 1)
        steps.append([d ^ (step if d & top == 0 else step + 1) for d in range(peers)])
    return steps


def inverse(step):
    back = [0] * len(step)
    for source, target in enumerate(step):
        back[target] = source
    return back


def after(array, *others):
    return lax.optimization_barrier((array, *others))[0]


def own_of(plan, column):
    return plan[2 + 3 * column]


def pick(blocks, partner, neighbours, rows, plan, columns, cost=SMALL):
    local_count, width, depth = blocks.shape
    count = len(columns)

    def lookup(row, index):
        value = row[0]
        for place, entry in enumerate(row[1:], 1):
            value = jnp.where(index == place, entry, value)
        return value

    def body(*refs):
        if plan is None:
            partners, kept, source = refs[:3]
            outs, made, into = refs[3 : 3 + count], refs[3 + count], refs[-1]
            me = lax.axis_index("orb").astype(jnp.int32)
            made[0] = me
            made[1] = lax.axis_index("aux").astype(jnp.int32)
            others = [lookup(row, me) for row in rows]
            for column in columns:
                made[2 + 3 * column] = partners[others[column], me]
        else:
            made, source = refs[:2]
            outs, into = refs[2 : 2 + count], refs[-1]
        reads = []
        for number, column in enumerate(columns):
            reads.append(
                pltpu.make_async_copy(
                    source.at[own_of(made, column)], outs[number], into.at[number]
                )
            )
        for read in reads:
            read.start()
        if plan is None:
            for column, other in enumerate(others):
                made[2 + 3 * column] = partners[other, me]
                made[3 + 3 * column] = other * local_count + partners[me, other]
                made[4 + 3 * column] = kept[me, other]
        for read in reads:
            read.wait()

    anywhere = pl.BlockSpec(memory_space=pl.ANY)
    out_specs = [pl.BlockSpec(memory_space=pltpu.VMEM)] * count
    near = count * width * depth * blocks.dtype.itemsize <= 4 * 1024 * 1024
    place = pltpu.VMEM if near else jax.ShapeDtypeStruct
    out_shape = [place((width, depth), blocks.dtype)] * count
    if plan is None:
        out_specs.append(pl.BlockSpec(memory_space=pltpu.SMEM))
        out_shape.append(jax.ShapeDtypeStruct((2 + 3 * len(rows),), jnp.int32))
    scalars = (partner, neighbours) if plan is None else (plan,)
    return pl.pallas_call(
        body,
        grid_spec=pltpu.PrefetchScalarGridSpec(
            num_scalar_prefetch=len(scalars),
            in_specs=[anywhere],
            out_specs=out_specs,
            scratch_shapes=[pltpu.SemaphoreType.DMA((count,))],
        ),
        out_shape=out_shape,
        compiler_params=PARAMS,
        cost_estimate=cost,
        name="pick",
    )(*scalars, blocks)


def kernel_parts(own, far, shards, sent):
    width = own[0].shape[0]
    rows = width // shards
    turn = lax.axis_index("aux").astype(jnp.int32)
    kernels = []
    for mine, other in zip(own, far):
        other = mine if other is None else other
        kernels.append(jnp.einsum("ap,bp->ab", mine, other, preferred_element_type=jnp.float32))
    stacked = jnp.stack(kernels)
    parts = []
    for j in range(shards):
        start = lax.rem(turn + j, shards) * rows
        part = lax.dynamic_slice_in_dim(stacked, start, rows, 1)
        parts.append(part.astype(sent) if j else part)
    return parts


def denominators(excitation, plan, column_groups, shards, local_count):
    width = excitation.shape[1]
    rows = width // shards
    count = len(column_groups)

    def body(plan, energies, *refs):
        outs, turned = refs[:count], refs[count]
        turned[...] = energies[...].T
        own_part = turned[pl.ds(pl.multiple_of(plan[1] * rows, rows), rows), :]
        lane = lax.broadcasted_iota(jnp.int32, own_part.shape, 1)
        for out, columns in zip(outs, column_groups):
            for pair, column in enumerate(columns):
                own = plan[0] * local_count + own_of(plan, column)
                left = jnp.sum(jnp.where(lane == own, own_part, 0.0), axis=1, keepdims=True)
                right = energies[pl.ds(plan[3 + 3 * column], 1), :]
                kept = plan[4 + 3 * column].astype(jnp.float32)
                out[pair] = jnp.where(kept > 0, left + right, jnp.inf)

    shapes = [(len(columns), rows, width) for columns in column_groups]
    return pl.pallas_call(
        body,
        grid_spec=pltpu.PrefetchScalarGridSpec(
            num_scalar_prefetch=1,
            grid=(1,),
            in_specs=[pl.BlockSpec(excitation.shape, lambda i, plan: (0, 0))],
            out_specs=[pl.BlockSpec(shape, lambda i, plan: (0, 0, 0)) for shape in shapes],
            scratch_shapes=[pltpu.VMEM(excitation.shape[::-1], jnp.float32)],
        ),
        out_shape=[jax.ShapeDtypeStruct(shape, jnp.float32) for shape in shapes],
        cost_estimate=SMALL,
        name="denominators",
    )(plan, excitation)


def amplitudes(parts, denominator):
    kernel = parts[0]
    for part in parts[1:]:
        kernel = kernel + part.astype(jnp.float32)
    return (-kernel / denominator).astype(jnp.bfloat16)


def assemble(shard_refs, pair, turn, scratch, shards):
    rows = shard_refs[0].shape[1]
    for j in range(shards):
        start = pl.multiple_of(lax.rem(turn + shards - j, shards) * rows, rows)
        scratch[pl.ds(start, rows), :] = shard_refs[j][pair]


def whole_spec(array):
    zeros = (0,) * array.ndim
    return pl.BlockSpec(array.shape, lambda i, plan: zeros)


def accumulate(blocks, before, items, groups, plan, shards, kind):
    local_count, width, depth = blocks.shape
    pairs = len(items)
    step = 768 if depth % 768 == 0 and pairs < 16 else 256
    arrived = [item[0] for item in items if item[0] is not None]
    local = len(arrived) < pairs
    flat = [shard for group in groups for shard in group]

    def body(plan, *refs):
        refs = list(refs)
        own_ref = refs.pop(0) if local else None
        sums = None if before is None else refs.pop(0)
        others = [refs.pop(0) for _ in arrived]
        held = [[refs.pop(0) for _ in group] for group in groups]
        out, total, amps, spare = refs

        @pl.when(pl.program_id(0) == 0)
        def _():
            for number, (block, column, group, pair, transposed) in enumerate(items):
                if transposed:
                    assemble(held[group], pair, plan[1], spare, shards)
                    amps[number] = spare[...].T
                else:
                    assemble(held[group], pair, plan[1], amps.at[number], shards)

        total[...] = jnp.zeros_like(total) if sums is None else sums[...]
        for number, (block, column, group, pair, transposed) in enumerate(items):
            factor = own_ref[0] if block is None else others.pop(0)[...]
            total[own_of(plan, column)] += jnp.dot(
                amps[number], factor, preferred_element_type=jnp.float32
            )
        out[...] = total[...].astype(out.dtype)

    own_spec = pl.BlockSpec((1, width, step), lambda i, plan: (own_of(plan, 0), 0, i))
    far_spec = pl.BlockSpec((width, step), lambda i, plan: (0, i))
    all_spec = pl.BlockSpec((local_count, width, step), lambda i, plan: (0, 0, i))
    return pl.pallas_call(
        body,
        grid_spec=pltpu.PrefetchScalarGridSpec(
            num_scalar_prefetch=1,
            grid=(depth // step,),
            in_specs=[own_spec] * local
            + [all_spec] * (before is not None)
            + [far_spec] * len(arrived)
            + [whole_spec(shard) for shard in flat],
            out_specs=all_spec,
            scratch_shapes=[
                pltpu.VMEM((local_count, width, step), jnp.float32),
                pltpu.VMEM((pairs, width, width), jnp.bfloat16),
                pltpu.VMEM((width, width), jnp.bfloat16),
            ],
        ),
        out_shape=jax.ShapeDtypeStruct(blocks.shape, kind),
        compiler_params=PARAMS,
        cost_estimate=SMALL,
        name="accumulate",
    )(
        plan,
        *([blocks] if local else []),
        *([] if before is None else [before]),
        *arrived,
        *flat,
    )


def on_device(blocks, excitation, partner, neighbours):
    peers = lax.axis_size("orb")
    shards = lax.axis_size("aux")
    local_count = blocks.shape[0]
    forward = forward_steps(peers)
    count = len(forward)
    backward = [inverse(step) for step in forward]
    mate = [d ^ 1 for d in range(peers)]
    from_step = [2 + i for i in range(count)]
    to_step = [2 + count + i for i in range(count)]
    rows = [list(range(peers)), mate] + backward + forward
    def around(array, shift):
        return lax.ppermute(array, "aux", [(i, (i + shift) % shards) for i in range(shards)])

    def send(array, step):
        return lax.ppermute(array, "orb", list(enumerate(step)))

    moves, columns = [mate, forward[0]], [1, to_step[0]]
    for i in range(1, count):
        moves += [forward[i], backward[i]]
        columns += [to_step[i], from_step[i]]
    moves.append(backward[0])
    columns.append(from_step[0])
    picked = pick(blocks, partner, neighbours, rows, None, [*columns[:3], 0])
    *picked, local, plan = picked
    picked += pick(blocks, None, None, rows, plan, columns[3:])
    own = dict(zip([*columns, 0], [*picked, local]))

    size = 1 if count <= 3 else 4
    step_groups = [list(range(i, min(i + size, count))) for i in range(1, count, size)]
    column_groups = [[0, 1], [from_step[0]]]
    for steps in step_groups:
        column_groups.append([c for i in steps for c in (from_step[i], to_step[i])])
    energies = denominators(excitation, plan, column_groups, shards, local_count)

    def reduced(far, columns, sent):
        parts = kernel_parts([own[column] for column in columns], far, shards, sent)
        return parts, [parts[0]] + [around(parts[j], j) for j in range(1, shards)]

    def spread(array):
        return [array] + [around(array, j) for j in range(1, shards)]

    received = [send(picked[number], moves[number]) for number in range(3)]

    def move(*gates):
        number = len(received)
        block = after(picked[number], received[number - WINDOW], *gates)
        received.append(send(block, moves[number]))

    parts, held = reduced([None, received[0]], [0, 1], jnp.float32)
    local = amplitudes(held, energies[0])
    move(*held[1:], *energies, *picked)
    far = after(received[1], local, *energies, *picked)
    parts, held = reduced([far], [from_step[0]], jnp.bfloat16)
    mine = amplitudes(held, energies[1])
    theirs = send(mine, backward[0])
    groups = [spread(after(local, *held[1:]))]
    move(theirs)
    waiting = [mine, theirs]
    items = [
        (None, 0, 0, 0, False),
        (received[0], 1, 0, 1, False),
        (received[1], from_step[0], 1, 0, False),
        (None, to_step[0], 1, 1, True),
    ]
    gates = groups[0][1:]
    for number, steps in enumerate(step_groups):
        columns = column_groups[2 + number]
        while len(received) < 2 + 2 * steps[-1]:
            move()
        far = [block for i in steps for block in received[2 * i : 2 * i + 2]]
        far = [after(block, *gates) for block in far]
        parts, held = reduced(far, columns, jnp.bfloat16)
        while len(received) < len(moves) - 1:
            move()
        amplitude = amplitudes(held, energies[2 + number])
        for place, column in enumerate(columns):
            items.append((far[place], column, 1 + number, len(waiting) + place, False))
        group = jnp.concatenate([*waiting, amplitude])
        groups.append(spread(group))
        if number == 0:
            move(amplitude)
        waiting = []
        gates = [group, *groups[-1][1:3]]
    items[3] = (received[-1], *items[3][1:])
    items = items[:3] + items[4:] + [items[3]]
    return accumulate(blocks, None, items, groups, plan, shards, jnp.bfloat16)


def solution(mesh):
    placed = (P("orb", None, "aux"), P(), P(), P())
    return jax.shard_map(
        on_device, mesh=mesh, in_specs=placed, out_specs=P("orb", None, "aux"), check_vma=False
    )
```

```python
import jax
import jax.numpy as jnp
from jax import lax
from jax.experimental import pallas as pl
from jax.experimental.pallas import tpu as pltpu
from jax.sharding import PartitionSpec as P

VMEM_BYTES = 56 * 1024 * 1024
WINDOW = 2
SMALL = pl.CostEstimate(flops=1, transcendentals=0, bytes_accessed=1)
LARGE = pl.CostEstimate(flops=1, transcendentals=0, bytes_accessed=60_000_000)
PARAMS = pltpu.CompilerParams(vmem_limit_bytes=VMEM_BYTES)


def forward_steps(peers):
    if peers == 8:
        ring = [0, 1, 3, 2]
        around = []
        for d in range(peers):
            place = ring.index(d >> 1)
            turn = 1 if d & 1 == 0 else 3
            around.append(ring[(place + turn) % 4] * 2 + (d & 1))
        crossed = [d ^ (3 if d & 1 == 0 else 5) for d in range(peers)]
        return [[d ^ (6 if d & 4 == 0 else 7) for d in range(peers)], crossed, around]
    steps = []
    for step in range(2, peers, 2):
        top = 1 << (step.bit_length() - 1)
        steps.append([d ^ (step if d & top == 0 else step + 1) for d in range(peers)])
    return steps


def inverse(step):
    back = [0] * len(step)
    for source, target in enumerate(step):
        back[target] = source
    return back


def after(array, *others):
    return lax.optimization_barrier((array, *others))[0]


def own_of(plan, column):
    return plan[2 + 3 * column]


def pick(blocks, partner, neighbours, rows, plan, columns, cost=SMALL):
    local_count, width, depth = blocks.shape
    count = len(columns)

    def lookup(row, index):
        value = row[0]
        for place, entry in enumerate(row[1:], 1):
            value = jnp.where(index == place, entry, value)
        return value

    def body(*refs):
        if plan is None:
            partners, kept, source = refs[:3]
            outs, made, into = refs[3 : 3 + count], refs[3 + count], refs[-1]
            me = lax.axis_index("orb").astype(jnp.int32)
            made[0] = me
            made[1] = lax.axis_index("aux").astype(jnp.int32)
            others = [lookup(row, me) for row in rows]
            for column in columns:
                made[2 + 3 * column] = partners[others[column], me]
        else:
            made, source = refs[:2]
            outs, into = refs[2 : 2 + count], refs[-1]
        reads = []
        for number, column in enumerate(columns):
            reads.append(
                pltpu.make_async_copy(
                    source.at[own_of(made, column)], outs[number], into.at[number]
                )
            )
        for read in reads:
            read.start()
        if plan is None:
            for column, other in enumerate(others):
                made[2 + 3 * column] = partners[other, me]
                made[3 + 3 * column] = other * local_count + partners[me, other]
                made[4 + 3 * column] = kept[me, other]
        for read in reads:
            read.wait()

    anywhere = pl.BlockSpec(memory_space=pl.ANY)
    out_specs = [pl.BlockSpec(memory_space=pltpu.VMEM)] * count
    near = count * width * depth * blocks.dtype.itemsize <= 4 * 1024 * 1024
    place = pltpu.VMEM if near else jax.ShapeDtypeStruct
    out_shape = [place((width, depth), blocks.dtype)] * count
    if plan is None:
        out_specs.append(pl.BlockSpec(memory_space=pltpu.SMEM))
        out_shape.append(jax.ShapeDtypeStruct((2 + 3 * len(rows),), jnp.int32))
    scalars = (partner, neighbours) if plan is None else (plan,)
    return pl.pallas_call(
        body,
        grid_spec=pltpu.PrefetchScalarGridSpec(
            num_scalar_prefetch=len(scalars),
            in_specs=[anywhere],
            out_specs=out_specs,
            scratch_shapes=[pltpu.SemaphoreType.DMA((count,))],
        ),
        out_shape=out_shape,
        compiler_params=PARAMS,
        cost_estimate=cost,
        name="pick",
    )(*scalars, blocks)


def kernel_parts(own, far, shards, sent):
    width = own[0].shape[0]
    rows = width // shards
    turn = lax.axis_index("aux").astype(jnp.int32)
    kernels = []
    for mine, other in zip(own, far):
        other = mine if other is None else other
        kernels.append(jnp.einsum("ap,bp->ab", mine, other, preferred_element_type=jnp.float32))
    stacked = jnp.stack(kernels)
    parts = []
    for j in range(shards):
        start = lax.rem(turn + j, shards) * rows
        part = lax.dynamic_slice_in_dim(stacked, start, rows, 1)
        parts.append(part.astype(sent) if j else part)
    return parts


def denominators(excitation, plan, column_groups, shards, local_count):
    width = excitation.shape[1]
    rows = width // shards
    count = len(column_groups)

    def body(plan, energies, *refs):
        outs, turned = refs[:count], refs[count]
        turned[...] = energies[...].T
        own_part = turned[pl.ds(pl.multiple_of(plan[1] * rows, rows), rows), :]
        lane = lax.broadcasted_iota(jnp.int32, own_part.shape, 1)
        for out, columns in zip(outs, column_groups):
            for pair, column in enumerate(columns):
                own = plan[0] * local_count + own_of(plan, column)
                left = jnp.sum(jnp.where(lane == own, own_part, 0.0), axis=1, keepdims=True)
                right = energies[pl.ds(plan[3 + 3 * column], 1), :]
                kept = plan[4 + 3 * column].astype(jnp.float32)
                out[pair] = jnp.where(kept > 0, left + right, jnp.inf)

    shapes = [(len(columns), rows, width) for columns in column_groups]
    return pl.pallas_call(
        body,
        grid_spec=pltpu.PrefetchScalarGridSpec(
            num_scalar_prefetch=1,
            grid=(1,),
            in_specs=[pl.BlockSpec(excitation.shape, lambda i, plan: (0, 0))],
            out_specs=[pl.BlockSpec(shape, lambda i, plan: (0, 0, 0)) for shape in shapes],
            scratch_shapes=[pltpu.VMEM(excitation.shape[::-1], jnp.float32)],
        ),
        out_shape=[jax.ShapeDtypeStruct(shape, jnp.float32) for shape in shapes],
        cost_estimate=SMALL,
        name="denominators",
    )(plan, excitation)


def amplitudes(parts, denominator):
    kernel = parts[0]
    for part in parts[1:]:
        kernel = kernel + part.astype(jnp.float32)
    return (-kernel / denominator).astype(jnp.bfloat16)


def assemble(shard_refs, pair, turn, scratch, shards):
    rows = shard_refs[0].shape[1]
    for j in range(shards):
        start = pl.multiple_of(lax.rem(turn + shards - j, shards) * rows, rows)
        scratch[pl.ds(start, rows), :] = shard_refs[j][pair]


def whole_spec(array):
    zeros = (0,) * array.ndim
    return pl.BlockSpec(array.shape, lambda i, plan: zeros)


def accumulate(blocks, before, items, groups, plan, shards, kind):
    local_count, width, depth = blocks.shape
    pairs = len(items)
    step = 768 if depth % 768 == 0 and pairs < 16 else 256
    arrived = [item[0] for item in items if item[0] is not None]
    local = len(arrived) < pairs
    flat = [shard for group in groups for shard in group]

    def body(plan, *refs):
        refs = list(refs)
        own_ref = refs.pop(0) if local else None
        sums = None if before is None else refs.pop(0)
        others = [refs.pop(0) for _ in arrived]
        held = [[refs.pop(0) for _ in group] for group in groups]
        out, total, amps, spare = refs

        @pl.when(pl.program_id(0) == 0)
        def _():
            for number, (block, column, group, pair, transposed) in enumerate(items):
                if transposed:
                    assemble(held[group], pair, plan[1], spare, shards)
                    amps[number] = spare[...].T
                else:
                    assemble(held[group], pair, plan[1], amps.at[number], shards)

        total[...] = jnp.zeros_like(total) if sums is None else sums[...]
        for number, (block, column, group, pair, transposed) in enumerate(items):
            factor = own_ref[0] if block is None else others.pop(0)[...]
            total[own_of(plan, column)] += jnp.dot(
                amps[number], factor, preferred_element_type=jnp.float32
            )
        out[...] = total[...].astype(out.dtype)

    own_spec = pl.BlockSpec((1, width, step), lambda i, plan: (own_of(plan, 0), 0, i))
    far_spec = pl.BlockSpec((width, step), lambda i, plan: (0, i))
    all_spec = pl.BlockSpec((local_count, width, step), lambda i, plan: (0, 0, i))
    return pl.pallas_call(
        body,
        grid_spec=pltpu.PrefetchScalarGridSpec(
            num_scalar_prefetch=1,
            grid=(depth // step,),
            in_specs=[own_spec] * local
            + [all_spec] * (before is not None)
            + [far_spec] * len(arrived)
            + [whole_spec(shard) for shard in flat],
            out_specs=all_spec,
            scratch_shapes=[
                pltpu.VMEM((local_count, width, step), jnp.float32),
                pltpu.VMEM((pairs, width, width), jnp.bfloat16),
                pltpu.VMEM((width, width), jnp.bfloat16),
            ],
        ),
        out_shape=jax.ShapeDtypeStruct(blocks.shape, kind),
        compiler_params=PARAMS,
        cost_estimate=SMALL,
        name="accumulate",
    )(
        plan,
        *([blocks] if local else []),
        *([] if before is None else [before]),
        *arrived,
        *flat,
    )


def on_device(blocks, excitation, partner, neighbours):
    peers = lax.axis_size("orb")
    shards = lax.axis_size("aux")
    local_count = blocks.shape[0]
    forward = forward_steps(peers)
    count = len(forward)
    backward = [inverse(step) for step in forward]
    mate = [d ^ 1 for d in range(peers)]
    from_step = [2 + i for i in range(count)]
    to_step = [2 + count + i for i in range(count)]
    rows = [list(range(peers)), mate] + backward + forward
    def around(array, shift):
        return lax.ppermute(array, "aux", [(i, (i + shift) % shards) for i in range(shards)])

    def send(array, step):
        return lax.ppermute(array, "orb", list(enumerate(step)))

    moves, columns = [mate, forward[0]], [1, to_step[0]]
    for i in range(1, count):
        moves += [forward[i], backward[i]]
        columns += [to_step[i], from_step[i]]
    moves.append(backward[0])
    columns.append(from_step[0])
    picked = pick(blocks, partner, neighbours, rows, None, [*columns[:3], 0])
    *picked, local, plan = picked
    picked += pick(blocks, None, None, rows, plan, columns[3:])
    own = dict(zip([*columns, 0], [*picked, local]))

    size = 1 if count <= 3 else 4
    step_groups = [list(range(i, min(i + size, count))) for i in range(1, count, size)]
    column_groups = [[0, 1], [from_step[0]]]
    for steps in step_groups:
        column_groups.append([c for i in steps for c in (from_step[i], to_step[i])])
    energies = denominators(excitation, plan, column_groups, shards, local_count)

    def reduced(far, columns, sent):
        parts = kernel_parts([own[column] for column in columns], far, shards, sent)
        return parts, [parts[0]] + [around(parts[j], j) for j in range(1, shards)]

    def spread(array):
        return [array] + [around(array, j) for j in range(1, shards)]

    received = [send(picked[number], moves[number]) for number in range(3)]

    def move(*gates):
        number = len(received)
        block = after(picked[number], received[number - WINDOW], *gates)
        received.append(send(block, moves[number]))

    parts, held = reduced([None, received[0]], [0, 1], jnp.float32)
    local = amplitudes(held, energies[0])
    move(*held[1:], *energies, *picked)
    far = after(received[1], local, *energies, *picked)
    parts, held = reduced([far], [from_step[0]], jnp.bfloat16)
    mine = amplitudes(held, energies[1])
    theirs = send(mine, backward[0])
    groups = [spread(after(local, *held[1:]))]
    move(theirs)
    waiting = [mine, theirs]
    items = [
        (None, 0, 0, 0, False),
        (received[0], 1, 0, 1, False),
        (received[1], from_step[0], 1, 0, False),
        (None, to_step[0], 1, 1, True),
    ]
    gates = groups[0][1:]
    for number, steps in enumerate(step_groups):
        columns = column_groups[2 + number]
        while len(received) < 2 + 2 * steps[-1]:
            move()
        far = [block for i in steps for block in received[2 * i : 2 * i + 2]]
        far = [after(block, *gates) for block in far]
        parts, held = reduced(far, columns, jnp.bfloat16)
        while len(received) < len(moves) - 1:
            move()
        amplitude = amplitudes(held, energies[2 + number])
        for place, column in enumerate(columns):
            items.append((far[place], column, 1 + number, len(waiting) + place, False))
        group = jnp.concatenate([*waiting, amplitude])
        groups.append(spread(group))
        if number == 0:
            move(amplitude, received[-1])
        waiting = []
        gates = [group, *groups[-1][1:3]]
    items[3] = (received[-1], *items[3][1:])
    items = items[:3] + items[4:] + [items[3]]
    return accumulate(blocks, None, items, groups, plan, shards, jnp.bfloat16)


def solution(mesh):
    placed = (P("orb", None, "aux"), P(), P(), P())
    return jax.shard_map(
        on_device, mesh=mesh, in_specs=placed, out_specs=P("orb", None, "aux"), check_vma=False
    )
```

```python
import jax
import jax.numpy as jnp
from jax import lax
from jax.experimental import pallas as pl
from jax.experimental.pallas import tpu as pltpu
from jax.sharding import PartitionSpec as P

VMEM_BYTES = 56 * 1024 * 1024
WINDOW = 2
SMALL = pl.CostEstimate(flops=1, transcendentals=0, bytes_accessed=1)
LARGE = pl.CostEstimate(flops=1, transcendentals=0, bytes_accessed=60_000_000)
PARAMS = pltpu.CompilerParams(vmem_limit_bytes=VMEM_BYTES)


def forward_steps(peers):
    if peers == 8:
        ring = [0, 1, 3, 2]
        around = []
        for d in range(peers):
            place = ring.index(d >> 1)
            turn = 1 if d & 1 == 0 else 3
            around.append(ring[(place + turn) % 4] * 2 + (d & 1))
        crossed = [d ^ (3 if d & 1 == 0 else 5) for d in range(peers)]
        return [[d ^ (6 if d & 4 == 0 else 7) for d in range(peers)], crossed, around]
    steps = []
    for step in range(2, peers, 2):
        top = 1 << (step.bit_length() - 1)
        steps.append([d ^ (step if d & top == 0 else step + 1) for d in range(peers)])
    return steps


def inverse(step):
    back = [0] * len(step)
    for source, target in enumerate(step):
        back[target] = source
    return back


def after(array, *others):
    return lax.optimization_barrier((array, *others))[0]


def own_of(plan, column):
    return plan[2 + 3 * column]


def pick(blocks, partner, neighbours, rows, plan, columns, cost=SMALL):
    local_count, width, depth = blocks.shape
    count = len(columns)

    def lookup(row, index):
        value = row[0]
        for place, entry in enumerate(row[1:], 1):
            value = jnp.where(index == place, entry, value)
        return value

    def body(*refs):
        if plan is None:
            partners, kept, source = refs[:3]
            outs, made, into = refs[3 : 3 + count], refs[3 + count], refs[-1]
            me = lax.axis_index("orb").astype(jnp.int32)
            made[0] = me
            made[1] = lax.axis_index("aux").astype(jnp.int32)
            others = [lookup(row, me) for row in rows]
            for column in columns:
                made[2 + 3 * column] = partners[others[column], me]
        else:
            made, source = refs[:2]
            outs, into = refs[2 : 2 + count], refs[-1]
        reads = []
        for number, column in enumerate(columns):
            reads.append(
                pltpu.make_async_copy(
                    source.at[own_of(made, column)], outs[number], into.at[number]
                )
            )
        for read in reads:
            read.start()
        if plan is None:
            for column, other in enumerate(others):
                made[2 + 3 * column] = partners[other, me]
                made[3 + 3 * column] = other * local_count + partners[me, other]
                made[4 + 3 * column] = kept[me, other]
        for read in reads:
            read.wait()

    anywhere = pl.BlockSpec(memory_space=pl.ANY)
    out_specs = [pl.BlockSpec(memory_space=pltpu.VMEM)] * count
    near = count * width * depth * blocks.dtype.itemsize <= 4 * 1024 * 1024
    place = pltpu.VMEM if near else jax.ShapeDtypeStruct
    out_shape = [place((width, depth), blocks.dtype)] * count
    if plan is None:
        out_specs.append(pl.BlockSpec(memory_space=pltpu.SMEM))
        out_shape.append(jax.ShapeDtypeStruct((2 + 3 * len(rows),), jnp.int32))
    scalars = (partner, neighbours) if plan is None else (plan,)
    return pl.pallas_call(
        body,
        grid_spec=pltpu.PrefetchScalarGridSpec(
            num_scalar_prefetch=len(scalars),
            in_specs=[anywhere],
            out_specs=out_specs,
            scratch_shapes=[pltpu.SemaphoreType.DMA((count,))],
        ),
        out_shape=out_shape,
        compiler_params=PARAMS,
        cost_estimate=cost,
        name="pick",
    )(*scalars, blocks)


def kernel_parts(own, far, shards, sent):
    width = own[0].shape[0]
    rows = width // shards
    turn = lax.axis_index("aux").astype(jnp.int32)
    kernels = []
    for mine, other in zip(own, far):
        other = mine if other is None else other
        kernels.append(jnp.einsum("ap,bp->ab", mine, other, preferred_element_type=jnp.float32))
    stacked = jnp.stack(kernels)
    parts = []
    for j in range(shards):
        start = lax.rem(turn + j, shards) * rows
        part = lax.dynamic_slice_in_dim(stacked, start, rows, 1)
        parts.append(part.astype(sent) if j else part)
    return parts


def denominators(excitation, plan, column_groups, shards, local_count):
    width = excitation.shape[1]
    rows = width // shards
    count = len(column_groups)

    def body(plan, energies, *refs):
        outs, turned = refs[:count], refs[count]
        turned[...] = energies[...].T
        own_part = turned[pl.ds(pl.multiple_of(plan[1] * rows, rows), rows), :]
        lane = lax.broadcasted_iota(jnp.int32, own_part.shape, 1)
        for out, columns in zip(outs, column_groups):
            for pair, column in enumerate(columns):
                own = plan[0] * local_count + own_of(plan, column)
                left = jnp.sum(jnp.where(lane == own, own_part, 0.0), axis=1, keepdims=True)
                right = energies[pl.ds(plan[3 + 3 * column], 1), :]
                kept = plan[4 + 3 * column].astype(jnp.float32)
                out[pair] = jnp.where(kept > 0, left + right, jnp.inf)

    shapes = [(len(columns), rows, width) for columns in column_groups]
    return pl.pallas_call(
        body,
        grid_spec=pltpu.PrefetchScalarGridSpec(
            num_scalar_prefetch=1,
            grid=(1,),
            in_specs=[pl.BlockSpec(excitation.shape, lambda i, plan: (0, 0))],
            out_specs=[pl.BlockSpec(shape, lambda i, plan: (0, 0, 0)) for shape in shapes],
            scratch_shapes=[pltpu.VMEM(excitation.shape[::-1], jnp.float32)],
        ),
        out_shape=[jax.ShapeDtypeStruct(shape, jnp.float32) for shape in shapes],
        cost_estimate=SMALL,
        name="denominators",
    )(plan, excitation)


def amplitudes(parts, denominator):
    kernel = parts[0]
    for part in parts[1:]:
        kernel = kernel + part.astype(jnp.float32)
    return (-kernel / denominator).astype(jnp.bfloat16)


def assemble(shard_refs, pair, turn, scratch, shards):
    rows = shard_refs[0].shape[1]
    for j in range(shards):
        start = pl.multiple_of(lax.rem(turn + shards - j, shards) * rows, rows)
        scratch[pl.ds(start, rows), :] = shard_refs[j][pair]


def whole_spec(array):
    zeros = (0,) * array.ndim
    return pl.BlockSpec(array.shape, lambda i, plan: zeros)


def accumulate(blocks, before, items, groups, plan, shards, kind):
    local_count, width, depth = blocks.shape
    pairs = len(items)
    step = 768 if depth % 768 == 0 and pairs < 16 else 256
    arrived = [item[0] for item in items if item[0] is not None]
    local = len(arrived) < pairs
    flat = [shard for group in groups for shard in group]

    def body(plan, *refs):
        refs = list(refs)
        own_ref = refs.pop(0) if local else None
        sums = None if before is None else refs.pop(0)
        others = [refs.pop(0) for _ in arrived]
        held = [[refs.pop(0) for _ in group] for group in groups]
        out, total, amps, spare = refs

        @pl.when(pl.program_id(0) == 0)
        def _():
            for number, (block, column, group, pair, transposed) in enumerate(items):
                if transposed:
                    assemble(held[group], pair, plan[1], spare, shards)
                    amps[number] = spare[...].T
                else:
                    assemble(held[group], pair, plan[1], amps.at[number], shards)

        total[...] = jnp.zeros_like(total) if sums is None else sums[...]
        for number, (block, column, group, pair, transposed) in enumerate(items):
            factor = own_ref[0] if block is None else others.pop(0)[...]
            total[own_of(plan, column)] += jnp.dot(
                amps[number], factor, preferred_element_type=jnp.float32
            )
        out[...] = total[...].astype(out.dtype)

    own_spec = pl.BlockSpec((1, width, step), lambda i, plan: (own_of(plan, 0), 0, i))
    far_spec = pl.BlockSpec((width, step), lambda i, plan: (0, i))
    all_spec = pl.BlockSpec((local_count, width, step), lambda i, plan: (0, 0, i))
    return pl.pallas_call(
        body,
        grid_spec=pltpu.PrefetchScalarGridSpec(
            num_scalar_prefetch=1,
            grid=(depth // step,),
            in_specs=[own_spec] * local
            + [all_spec] * (before is not None)
            + [far_spec] * len(arrived)
            + [whole_spec(shard) for shard in flat],
            out_specs=all_spec,
            scratch_shapes=[
                pltpu.VMEM((local_count, width, step), jnp.float32),
                pltpu.VMEM((pairs, width, width), jnp.bfloat16),
                pltpu.VMEM((width, width), jnp.bfloat16),
            ],
        ),
        out_shape=jax.ShapeDtypeStruct(blocks.shape, kind),
        compiler_params=PARAMS,
        cost_estimate=SMALL,
        name="accumulate",
    )(
        plan,
        *([blocks] if local else []),
        *([] if before is None else [before]),
        *arrived,
        *flat,
    )


def on_device(blocks, excitation, partner, neighbours):
    peers = lax.axis_size("orb")
    shards = lax.axis_size("aux")
    local_count = blocks.shape[0]
    forward = forward_steps(peers)
    count = len(forward)
    backward = [inverse(step) for step in forward]
    mate = [d ^ 1 for d in range(peers)]
    from_step = [2 + i for i in range(count)]
    to_step = [2 + count + i for i in range(count)]
    rows = [list(range(peers)), mate] + backward + forward
    def around(array, shift):
        return lax.ppermute(array, "aux", [(i, (i + shift) % shards) for i in range(shards)])

    def send(array, step):
        return lax.ppermute(array, "orb", list(enumerate(step)))

    moves, columns = [mate, forward[0]], [1, to_step[0]]
    for i in range(1, count):
        moves += [forward[i], backward[i]]
        columns += [to_step[i], from_step[i]]
    moves.append(backward[0])
    columns.append(from_step[0])
    picked = pick(blocks, partner, neighbours, rows, None, [*columns[:3], 0])
    *picked, local, plan = picked
    picked += pick(blocks, None, None, rows, plan, columns[3:])
    own = dict(zip([*columns, 0], [*picked, local]))

    size = 1 if count <= 3 else 4
    step_groups = [list(range(i, min(i + size, count))) for i in range(1, count, size)]
    column_groups = [[0, 1], [from_step[0]]]
    for steps in step_groups:
        column_groups.append([c for i in steps for c in (from_step[i], to_step[i])])
    energies = denominators(excitation, plan, column_groups, shards, local_count)

    def reduced(far, columns, sent):
        parts = kernel_parts([own[column] for column in columns], far, shards, sent)
        return parts, [parts[0]] + [around(parts[j], j) for j in range(1, shards)]

    def spread(array):
        return [array] + [around(array, j) for j in range(1, shards)]

    received = [send(picked[number], moves[number]) for number in range(3)]

    def move(*gates):
        number = len(received)
        block = after(picked[number], received[number - WINDOW], *gates)
        received.append(send(block, moves[number]))

    parts, held = reduced([None, received[0]], [0, 1], jnp.float32)
    local = amplitudes(held, energies[0])
    move(*held[1:], *energies, *picked)
    far = after(received[1], local, *energies, *picked)
    parts, held = reduced([far], [from_step[0]], jnp.bfloat16)
    mine = amplitudes(held, energies[1])
    theirs = send(mine, backward[0])
    groups = [spread(after(local, mine))]
    move(theirs)
    waiting = [mine, theirs]
    items = [
        (None, 0, 0, 0, False),
        (received[0], 1, 0, 1, False),
        (received[1], from_step[0], 1, 0, False),
        (None, to_step[0], 1, 1, True),
    ]
    gates = groups[0][1:]
    for number, steps in enumerate(step_groups):
        columns = column_groups[2 + number]
        while len(received) < 2 + 2 * steps[-1]:
            move()
        far = [block for i in steps for block in received[2 * i : 2 * i + 2]]
        far = [after(block, *gates) for block in far]
        parts, held = reduced(far, columns, jnp.bfloat16)
        while len(received) < len(moves) - 1:
            move()
        amplitude = amplitudes(held, energies[2 + number])
        for place, column in enumerate(columns):
            items.append((far[place], column, 1 + number, len(waiting) + place, False))
        group = jnp.concatenate([*waiting, amplitude])
        groups.append(spread(group))
        if number == 0:
            move(amplitude, received[-1])
        waiting = []
        gates = [group, *groups[-1][1:3]]
    items[3] = (received[-1], *items[3][1:])
    items = items[:3] + items[4:] + [items[3]]
    return accumulate(blocks, None, items, groups, plan, shards, jnp.bfloat16)


def solution(mesh):
    placed = (P("orb", None, "aux"), P(), P(), P())
    return jax.shard_map(
        on_device, mesh=mesh, in_specs=placed, out_specs=P("orb", None, "aux"), check_vma=False
    )
```
